32 devices in a mesh: grp: 8 (over y, x, core), blk: 4 (over z).
Axes of the slice: x: 2, y: 2, z: 4, core: 2. Of those that a mesh axis runs over, the one named last changes fastest.
Arguments:
- inputs: bfloat16 [8, 2, 1024, 640], P('grp', None, 'blk'), may hold values from -6 to 6
- cotangent: bfloat16 [8, 2, 1024, 640], P('grp', None, 'blk'), may hold values from -6 to 6
- master_attend: float32 [640, 1536], P('blk'), may hold values from -0.25 to 0.25
- master_merge: float32 [1024, 640], P('blk'), may hold values from -0.1875 to 0.1875
- master_expand: float32 [640, 4096], P('blk'), may hold values from -0.25 to 0.25
- master_reduce: float32 [2048, 640], P('blk'), may hold values from -0.125 to 0.125
- master_gains: float32 [3072], P('blk'), may hold values from -1 to 1
- moment_attend: float32 [640, 1536], P('blk'), may hold values from -3 to 3
- moment_merge: float32 [1024, 640], P('blk'), may hold values from -3 to 3
- moment_expand: float32 [640, 4096], P('blk'), may hold values from -3 to 3
- moment_reduce: float32 [2048, 640], P('blk'), may hold values from -3 to 3
- moment_gains: float32 [3072], P('blk'), may hold values from -3 to 3
- error_attend: float32 [8, 640, 1536], P('grp', 'blk'), may hold values from -192 to 192
- error_merge: float32 [8, 1024, 640], P('grp', 'blk'), may hold values from -192 to 192
- error_expand: float32 [8, 640, 4096], P('grp', 'blk'), may hold values from -192 to 192
- error_reduce: float32 [8, 2048, 640], P('grp', 'blk'), may hold values from -192 to 192
- start_attend: float32 [4, 1536, 8], P('blk'), may hold values from -6 to 6
- start_merge: float32 [4, 640, 8], P('blk'), may hold values from -6 to 6
- start_expand: float32 [4, 4096, 8], P('blk'), may hold values from -6 to 6
- start_reduce: float32 [4, 640, 8], P('blk'), may hold values from -6 to 6
Outputs:
- block_output: bfloat16 [8, 2, 1024, 640], P('grp', None, 'blk')
- input_grad: float32 [8, 2, 1024, 640], P('grp', None, 'blk')
- grad_attend: float32 [8, 640, 1536], P('grp', 'blk')
- grad_merge: float32 [8, 1024, 640], P('grp', 'blk')
- grad_expand: float32 [8, 640, 4096], P('grp', 'blk')
- grad_reduce: float32 [8, 2048, 640], P('grp', 'blk')
- grad_gains: float32 [8, 3072], P('grp', 'blk')
- left_attend: float32 [640, 8], P('blk')
- left_merge: float32 [1024, 8], P('blk')
- left_expand: float32 [640, 8], P('blk')
- left_reduce: float32 [2048, 8], P('blk')
- right_attend: float32 [4, 1536, 8], P('blk')
- right_merge: float32 [4, 640, 8], P('blk')
- right_expand: float32 [4, 4096, 8], P('blk')
- right_reduce: float32 [4, 640, 8], P('blk')
- residue_attend: float32 [8, 640, 1536], P('grp', 'blk')
- residue_merge: float32 [8, 1024, 640], P('grp', 'blk')
- residue_expand: float32 [8, 640, 4096], P('grp', 'blk')
- residue_reduce: float32 [8, 2048, 640], P('grp', 'blk')
- velocity_attend: float32 [640, 1536], P('blk')
- velocity_merge: float32 [1024, 640], P('blk')
- velocity_expand: float32 [640, 4096], P('blk')
- velocity_reduce: float32 [2048, 640], P('blk')
- velocity_gains: float32 [3072], P('blk')
- weight_attend: float32 [640, 1536], P('blk')
- weight_merge: float32 [1024, 640], P('blk')
- weight_expand: float32 [640, 4096], P('blk')
- weight_reduce: float32 [2048, 640], P('blk')
- weight_gains: float32 [3072], P('blk')
- copy_attend: bfloat16 [640, 1536], P('blk')
- copy_merge: bfloat16 [1024, 640], P('blk')
- copy_expand: bfloat16 [640, 4096], P('blk')
- copy_reduce: bfloat16 [2048, 640], P('blk')
- copy_gains: bfloat16 [3072], P('blk')
The draws below stay inside these ranges and needn't reach their ends.
All inputs are finite; a program needn't handle non-finite values.
Results may differ from the reference program's by a relative error of at most 0.028.
Values may be sent and summed in bfloat16 or wider, within the bound.
No kernel may reach another device: no remote copies, remote signals or barrier semaphores. Data moves between devices by JAX's collectives and lax.ppermute only.
A program may use at most 192 MiB of HBM per device.

```python
import jax
import jax.numpy as jnp
from jax import lax

D = 640
NH = 4
HD = 256
FF = 2048
WINDOW = 512
RANK = 8
SEG = 256
HQ = 1024
QKV = 1536
GAINS = 3072
PROMPT = 1024
GROUPS = 8
N_BLK = 4


def steps_of(own_key, dims, shards, low, high):
    loudness, own = 1.0, jax.random.fold_in(own_key, 6)
    for position, blocks in shards:
        heights = jnp.exp(jax.random.uniform(jax.random.fold_in(own, position), (blocks,), jnp.float32, low / len(shards), high / len(shards)))
        loudness = loudness * jnp.repeat(heights, dims[position] // blocks).reshape([-1 if axis == position else 1 for axis in range(len(dims))])
    return loudness


def normal_values(key, extent, width, bound, pieces=(), kind=jnp.bfloat16):
    gain = steps_of(key, extent, pieces, -0.22, 0.18) if pieces else 1.0
    drawn = jax.random.normal(key, extent, jnp.float32) * width * gain
    return jnp.minimum(jnp.maximum(drawn, -bound), bound).astype(kind)


def setup_inputs(seed: int = 0) -> dict:
    streams_of = jax.random.split(jax.random.key(seed), 21)
    inputs = normal_values(streams_of[0], (GROUPS, 2, PROMPT, D), 1.0, 6.0, ((0, 8), (2, 4)))
    cotangent = normal_values(streams_of[1], (GROUPS, 2, PROMPT, D), 1.0, 6.0, ((0, 8), (2, 4)))
    master_attend = normal_values(streams_of[2], (D, QKV), D ** -0.5, 0.25, ((0, 4),), jnp.float32)
    master_merge = normal_values(streams_of[3], (HQ, D), HQ ** -0.5, 0.1875, ((0, 4),), jnp.float32)
    master_expand = normal_values(streams_of[4], (D, 2 * FF), D ** -0.5, 0.25, ((0, 4),), jnp.float32)
    master_reduce = normal_values(streams_of[5], (FF, D), FF ** -0.5, 0.125, ((0, 4),), jnp.float32)
    master_gains = normal_values(streams_of[6], (GAINS,), 0.2, 1.0, ((0, 4),), jnp.float32)
    moment_attend = normal_values(streams_of[7], (D, QKV), 0.5, 3.0, ((0, 4),), jnp.float32)
    moment_merge = normal_values(streams_of[8], (HQ, D), 0.5, 3.0, ((0, 4),), jnp.float32)
    moment_expand = normal_values(streams_of[9], (D, 2 * FF), 0.5, 3.0, ((0, 4),), jnp.float32)
    moment_reduce = normal_values(streams_of[10], (FF, D), 0.5, 3.0, ((0, 4),), jnp.float32)
    moment_gains = normal_values(streams_of[11], (GAINS,), 0.5, 3.0, ((0, 4),), jnp.float32)
    error_attend = normal_values(streams_of[12], (GROUPS, D, QKV), 32.0, 192.0, ((0, 8), (1, 4)), jnp.float32)
    error_merge = normal_values(streams_of[13], (GROUPS, HQ, D), 32.0, 192.0, ((0, 8), (1, 4)), jnp.float32)
    error_expand = normal_values(streams_of[14], (GROUPS, D, 2 * FF), 32.0, 192.0, ((0, 8), (1, 4)), jnp.float32)
    error_reduce = normal_values(streams_of[15], (GROUPS, FF, D), 32.0, 192.0, ((0, 8), (1, 4)), jnp.float32)
    start_attend = normal_values(streams_of[16], (N_BLK, QKV, RANK), 1.0, 6.0, ((0, 4),), jnp.float32)
    start_merge = normal_values(streams_of[17], (N_BLK, D, RANK), 1.0, 6.0, ((0, 4),), jnp.float32)
    start_expand = normal_values(streams_of[18], (N_BLK, 2 * FF, RANK), 1.0, 6.0, ((0, 4),), jnp.float32)
    start_reduce = normal_values(streams_of[19], (N_BLK, D, RANK), 1.0, 6.0, ((0, 4),), jnp.float32)
    return {"inputs": inputs, "cotangent": cotangent, "master_attend": master_attend, "master_merge": master_merge, "master_expand": master_expand, "master_reduce": master_reduce, "master_gains": master_gains, "moment_attend": moment_attend, "moment_merge": moment_merge, "moment_expand": moment_expand, "moment_reduce": moment_reduce, "moment_gains": moment_gains, "error_attend": error_attend, "error_merge": error_merge, "error_expand": error_expand, "error_reduce": error_reduce, "start_attend": start_attend, "start_merge": start_merge, "start_expand": start_expand, "start_reduce": start_reduce}


NORM_EPS = 1e-06
ROPE_BASE = 10000.0
ERROR_KEEP = 0.5
MOMENTUM = 0.9
STEP_RATE = 0.02
NEG_FILL = -1e+30

@jax.custom_vjp
def low(v):
    return lax.optimization_barrier(v.astype(jnp.bfloat16)).astype(jnp.float32)

@jax.custom_vjp
def reduced_backward(v):
    return v

def low_keep(v):
    return (low(v), None)

def low_pass(kept, grad):
    return (grad,)

def back_keep(v):
    return (v, None)

def back_low(kept, grad):
    return (low(grad),)
low.defvjp(low_keep, low_pass)
reduced_backward.defvjp(back_keep, back_low)

def rmsnorm(values, gain_row):
    return values * lax.rsqrt(lax.optimization_barrier(jnp.mean(values * values, axis=-1, keepdims=True)) + NORM_EPS) * (1.0 + gain_row)

def rotate(values, cosine, sine_part):
    middle = values.shape[-1] // 2
    turned = jnp.concatenate([-values[..., middle:], values[..., :middle]], axis=-1)
    return values * cosine + turned * sine_part

def rope_tables(places):
    frequency = jnp.arange(HD // 2, dtype=jnp.float32)
    inverse = ROPE_BASE ** (-2.0 * frequency / HD)
    angles = places.astype(jnp.float32)[:, None] * inverse[None, :]
    angles = jnp.concatenate([angles, angles], axis=-1)
    return (jnp.cos(angles), jnp.sin(angles))

def prepare_heads(projected, gain_query, gain_key, cosine, sine_part):
    row_count = projected.shape[0]
    query_rows = projected[:, :HQ].reshape(row_count, NH, HD)
    keys_raw = projected[:, HQ:HQ + HD]
    values_raw = projected[:, HQ + HD:]
    query_rows = rotate(rmsnorm(query_rows, gain_query), cosine[:, None, :], sine_part[:, None, :]) * HD ** (-0.5)
    keys_rot = rotate(rmsnorm(keys_raw, gain_key), cosine, sine_part)
    return (query_rows, keys_rot, values_raw)

def gated_gelu(gate_up):
    return jax.nn.gelu(gate_up[:, :FF], approximate=True) * gate_up[:, FF:]

def orthonormal(factor):
    columns = []
    for column in range(factor.shape[1]):
        vector = factor[:, column]
        for basis in columns:
            vector = vector - jnp.sum(basis * vector) * basis
        columns.append(vector * lax.rsqrt(jnp.sum(vector * vector) + NORM_EPS))
    return jnp.stack(columns, axis=1)

def attend_rows(query_rows, incoming_keys, incoming_values, allowed):
    attention_scores = reduced_backward(jnp.einsum('itge,iue->igtu', query_rows, incoming_keys, precision=lax.Precision.HIGHEST))
    attention_scores = jnp.where(allowed[:, None], attention_scores, NEG_FILL)
    top_score = lax.optimization_barrier(jnp.max(attention_scores, axis=-1, keepdims=True))
    expos = jnp.exp(attention_scores - top_score)
    attention_probabilities = low(expos / lax.optimization_barrier(jnp.sum(expos, axis=-1, keepdims=True)))
    return jnp.einsum('ayco,aox->acyx', attention_probabilities, incoming_values, precision=lax.Precision.HIGHEST)

def layer(rows_in, full_attend, full_merge, full_expand, full_reduce, gain_all):
    prompt_size = rows_in.shape[1]
    blocks = prompt_size // SEG
    gain_first = gain_all[:D]
    gain_second = gain_all[D:2 * D]
    gain_third = gain_all[2 * D:3 * D]
    gain_fourth = gain_all[3 * D:4 * D]
    gain_query = gain_all[4 * D:4 * D + HD]
    gain_key = gain_all[4 * D + HD:]
    flat = rows_in.reshape(2 * prompt_size, D)
    offsets = jnp.arange(prompt_size, dtype=jnp.int32)
    places = jnp.concatenate([offsets, prompt_size + offsets % SEG])
    cosine, sine_part = rope_tables(places)
    normed = low(rmsnorm(flat, gain_first))
    projected = reduced_backward(jnp.dot(normed, full_attend, precision=lax.Precision.HIGHEST))
    query_rows, keys_rot, values_raw = prepare_heads(projected, gain_query, gain_key, cosine, sine_part)
    query_rows = low(query_rows)
    keys_rot = low(keys_rot)
    values_raw = low(values_raw)
    distance = offsets[:, None] - offsets[None, :]
    prompt_mask = (distance >= 0) & (distance < WINDOW)
    prompt_out = attend_rows(query_rows[None, :prompt_size], keys_rot[None, :prompt_size], values_raw[None, :prompt_size], prompt_mask[None])
    reply_keys = jnp.concatenate([jnp.broadcast_to(keys_rot[None, prompt_size - WINDOW:prompt_size], (blocks, WINDOW, HD)), keys_rot[prompt_size:].reshape(blocks, SEG, HD)], axis=1)
    reply_values = jnp.concatenate([jnp.broadcast_to(values_raw[None, prompt_size - WINDOW:prompt_size], (blocks, WINDOW, HD)), values_raw[prompt_size:].reshape(blocks, SEG, HD)], axis=1)
    span = jnp.arange(WINDOW + SEG, dtype=jnp.int32)
    key_place = jnp.where(span < WINDOW, prompt_size - WINDOW + span, prompt_size + span - WINDOW)
    query_place = prompt_size + jnp.arange(SEG, dtype=jnp.int32)
    reply_gap = query_place[:, None] - key_place[None, :]
    reply_mask = (reply_gap >= 0) & (reply_gap < WINDOW)
    reply_out = attend_rows(query_rows[prompt_size:].reshape(blocks, SEG, NH, HD), reply_keys, reply_values, reply_mask[None])
    context = jnp.concatenate([prompt_out.reshape(prompt_size, HQ), reply_out.reshape(prompt_size, HQ)], axis=0)
    context = low(reduced_backward(context))
    branch_attn = reduced_backward(jnp.dot(context, full_merge, precision=lax.Precision.HIGHEST))
    hidden = flat + rmsnorm(branch_attn, gain_second)
    normed_mid = low(rmsnorm(hidden, gain_third))
    gate_up = reduced_backward(jnp.dot(normed_mid, full_expand, precision=lax.Precision.HIGHEST))
    activated = low(gated_gelu(gate_up))
    branch_ff = reduced_backward(jnp.dot(activated, full_reduce, precision=lax.Precision.HIGHEST))
    return (hidden + rmsnorm(branch_ff, gain_fourth)).reshape(2, prompt_size, D)

def compress(gradients, buffers, factors):
    group_count, row_count, column_count = gradients.shape
    combined = gradients + ERROR_KEEP * buffers
    blocked = combined.reshape(group_count, N_BLK, row_count // N_BLK, column_count)
    left_sum = jnp.einsum('gbrc,bck->brk', blocked, factors, precision=lax.Precision.HIGHEST)
    basis_set = jax.vmap(orthonormal)(left_sum)
    partial_right = jnp.einsum('gbrc,brk->gbck', blocked, basis_set, precision=lax.Precision.HIGHEST)
    right_sum = lax.optimization_barrier(jnp.sum(partial_right, axis=0))
    approx = jnp.einsum('brk,bck->brc', basis_set, right_sum, precision=lax.Precision.HIGHEST) / group_count
    residue = blocked - jnp.einsum('brk,gbck->gbrc', basis_set, partial_right, precision=lax.Precision.HIGHEST)
    return (approx.reshape(row_count, column_count), basis_set.reshape(row_count, RANK), right_sum, residue.reshape(group_count, row_count, column_count))

def reference(inputs, cotangent, master_attend, master_merge, master_expand, master_reduce, master_gains, moment_attend, moment_merge, moment_expand, moment_reduce, moment_gains, error_attend, error_merge, error_expand, error_reduce, start_attend, start_merge, start_expand, start_reduce):
    copy_attend = low(master_attend)
    copy_merge = low(master_merge)
    copy_expand = low(master_expand)
    copy_reduce = low(master_reduce)
    copy_gains = low(master_gains)

    def per_group(pair):
        group_in, group_cot = pair
        result, pullback = jax.vjp(layer, group_in.astype(jnp.float32), copy_attend, copy_merge, copy_expand, copy_reduce, copy_gains)
        grads_all = pullback(group_cot.astype(jnp.float32))
        return (result.astype(jnp.bfloat16), grads_all[0], grads_all[1], grads_all[2], grads_all[3], grads_all[4], grads_all[5])
    block_output, input_grad, grad_attend, grad_merge, grad_expand, grad_reduce, grad_gains = lax.map(per_group, (inputs, cotangent))
    approx_attend, left_attend, right_attend, residue_attend = compress(grad_attend, error_attend, start_attend)
    approx_merge, left_merge, right_merge, residue_merge = compress(grad_merge, error_merge, start_merge)
    approx_expand, left_expand, right_expand, residue_expand = compress(grad_expand, error_expand, start_expand)
    approx_reduce, left_reduce, right_reduce, residue_reduce = compress(grad_reduce, error_reduce, start_reduce)
    approx_gains = lax.optimization_barrier(jnp.sum(grad_gains, axis=0)) / GROUPS
    velocity_attend = MOMENTUM * moment_attend + (1.0 - MOMENTUM) * approx_attend
    velocity_merge = MOMENTUM * moment_merge + (1.0 - MOMENTUM) * approx_merge
    velocity_expand = MOMENTUM * moment_expand + (1.0 - MOMENTUM) * approx_expand
    velocity_reduce = MOMENTUM * moment_reduce + (1.0 - MOMENTUM) * approx_reduce
    velocity_gains = MOMENTUM * moment_gains + (1.0 - MOMENTUM) * approx_gains
    weight_attend = master_attend - STEP_RATE * velocity_attend
    weight_merge = master_merge - STEP_RATE * velocity_merge
    weight_expand = master_expand - STEP_RATE * velocity_expand
    weight_reduce = master_reduce - STEP_RATE * velocity_reduce
    weight_gains = master_gains - STEP_RATE * velocity_gains
    return (block_output, input_grad, grad_attend, grad_merge, grad_expand, grad_reduce, grad_gains, left_attend, left_merge, left_expand, left_reduce, right_attend, right_merge, right_expand, right_reduce, residue_attend, residue_merge, residue_expand, residue_reduce, velocity_attend, velocity_merge, velocity_expand, velocity_reduce, velocity_gains, weight_attend, weight_merge, weight_expand, weight_reduce, weight_gains, weight_attend.astype(jnp.bfloat16), weight_merge.astype(jnp.bfloat16), weight_expand.astype(jnp.bfloat16), weight_reduce.astype(jnp.bfloat16), weight_gains.astype(jnp.bfloat16))
```

```python
import jax
import jax.numpy as jnp
from jax import lax
from jax.experimental import pallas as pl
from jax.experimental.pallas import tpu as pltpu
from jax.sharding import PartitionSpec as P


D = 640
NH = 4
HD = 256
FF = 2048
WINDOW = 512
SEG = 256
HQ = 1024


NORM_EPS = 1e-06
ROPE_BASE = 10000.0
ERROR_KEEP = 0.5
MOMENTUM = 0.9
STEP_RATE = 0.02
NEG_FILL = -1e30


def rmsnorm(values, gain_row):
    return (
        values
        * lax.rsqrt(jnp.mean(values * values, axis=-1, keepdims=True) + NORM_EPS)
        * (1.0 + gain_row)
    )


def rotate(values, cosine, sine_part):
    middle = values.shape[-1] // 2
    turned = jnp.concatenate([-values[..., middle:], values[..., :middle]], axis=-1)
    return values * cosine + turned * sine_part


def rope_tables(places):
    frequency = jnp.arange(HD // 2, dtype=jnp.float32)
    inverse = ROPE_BASE ** (-2.0 * frequency / HD)
    angles = places.astype(jnp.float32)[:, None] * inverse[None, :]
    angles = jnp.concatenate([angles, angles], axis=-1)
    return (jnp.cos(angles), jnp.sin(angles))


def prepare_heads(projected, gain_query, gain_key, cosine, sine_part):
    row_count = projected.shape[0]
    query_rows = projected[:, :HQ].reshape(row_count, NH, HD)
    keys_raw = projected[:, HQ : HQ + HD]
    values_raw = projected[:, HQ + HD :]
    query_rows = rotate(
        rmsnorm(query_rows, gain_query), cosine[:, None, :], sine_part[:, None, :]
    ) * HD ** (-0.5)
    keys_rot = rotate(rmsnorm(keys_raw, gain_key), cosine, sine_part)
    return (query_rows, keys_rot, values_raw)


def gated_gelu(gate_up):
    return jax.nn.gelu(gate_up[:, :FF], approximate=True) * gate_up[:, FF:]


def contract_rows(left_side, right_side):
    return lax.dot_general(
        left_side, right_side, (((0,), (0,)), ((), ())), preferred_element_type=jnp.float32
    )


def contract_cols(left_side, right_side):
    return lax.dot_general(
        left_side, right_side, (((1,), (1,)), ((), ())), preferred_element_type=jnp.float32
    )


AXES = ("grp", "blk")


def exchange(values, axis, bit):
    size = lax.axis_size(axis)
    return lax.ppermute(values, axis, [(place, place ^ bit) for place in range(size)])


def bits_below(limit):
    bit = 1
    while bit < limit:
        yield bit
        bit *= 2


def relocate(values):
    groups, blocks = lax.axis_size("grp"), lax.axis_size("blk")
    half = blocks // 2
    pairs = []
    for group in range(groups):
        for block in range(blocks):
            target = (group // 2 * 2 + block // half, group % 2 * half + block % half)
            pairs.append((group * blocks + block, target[0] * blocks + target[1]))
    return lax.ppermute(values, AXES, pairs)


def sum_groups(values):
    for bit in bits_below(lax.axis_size("grp")):
        values = values + exchange(values, "grp", bit)
    return values


def assemble_kernel(row_parts, order, place_ref, own_ref, near_ref, far_ref, full_ref, sems):
    group, block = place_ref[0], place_ref[1]
    height, width = own_ref.shape
    blocks = full_ref.shape[0] // height
    tall, wide = near_ref.shape[-2:]
    copies = [
        pltpu.make_async_copy(
            own_ref, full_ref.at[pl.ds(pl.multiple_of(block * height, height), height)], sems.at[0]
        )
    ]
    for side, pieces in enumerate((near_ref, far_ref)):
        for spot, mask in enumerate(order):
            part = lax.bitwise_xor(group, mask + side)
            row_part, column_part = (part >> 2, part & 3) if row_parts == 2 else (part, 0)
            for step in range(1, blocks):
                start = lax.bitwise_xor(block, step) * height + row_part * tall
                target = full_ref.at[
                    pl.ds(pl.multiple_of(start, tall), tall),
                    pl.ds(pl.multiple_of(column_part * wide, wide), wide),
                ]
                copies.append(
                    pltpu.make_async_copy(
                        pieces.at[spot, step - 1], target, sems.at[len(copies)]
                    )
                )
    for copy in copies:
        copy.start()
    for copy in copies:
        copy.wait()


def gather_rows(own, row_parts, first, place):
    blocks = lax.axis_size("blk")
    height, width = own.shape
    part = place[0]
    if row_parts == 2:
        tall, wide = height // 2, width // 4
        mine = lax.dynamic_slice(own, ((part >> 2) * tall, (part & 3) * wide), (tall, wide))
    else:
        tall, wide = height // 8, width
        mine = lax.dynamic_slice(own, (part * tall, 0), (tall, wide))
    held = mine[None]
    for bit in bits_below(blocks):
        held = jnp.concatenate([held, exchange(held, "blk", bit)])
    held = held[None, 1:]
    second = 6 - first
    held = jnp.concatenate([held, exchange(held, "grp", first)])
    held = jnp.concatenate([held, exchange(held, "grp", second)])
    far = exchange(held, "grp", 1)
    order = (0, first, second, first + second)
    return pl.pallas_call(
        lambda *refs: assemble_kernel(row_parts, order, *refs),
        out_shape=jax.ShapeDtypeStruct((blocks * height, width), own.dtype),
        in_specs=[pl.BlockSpec(memory_space=pltpu.SMEM)] + [pl.BlockSpec(memory_space=pl.ANY)] * 3,
        out_specs=pl.BlockSpec(memory_space=pltpu.VMEM),
        scratch_shapes=[pltpu.SemaphoreType.DMA((1 + 8 * (blocks - 1),))],
    )(place, own, held, far)


def orthonormal_kernel(*refs):
    count = len(refs) // 2
    factors = [ref[...] for ref in refs[:count]]
    rows = lax.broadcasted_iota(jnp.int32, (factors[0].shape[0], 1), 0)
    for column in range(factors[0].shape[0]):
        for member in range(count):
            factor = factors[member]
            vector = factor[column : column + 1]
            inner = jnp.sum(factor * vector, axis=1, keepdims=True)
            scale = lax.rsqrt(inner[column : column + 1] + NORM_EPS)
            basis = vector * scale
            weights = jnp.where(rows > column, inner * scale, 0.0)
            factors[member] = jnp.where(rows == column, basis, factor - weights * basis)
    for member in range(count):
        refs[count + member][...] = factors[member]


def orthonormal(factors):
    spec = pl.BlockSpec(memory_space=pltpu.VMEM)
    return pl.pallas_call(
        orthonormal_kernel,
        out_shape=[jax.ShapeDtypeStruct(factor.shape, factor.dtype) for factor in factors],
        in_specs=[spec] * len(factors),
        out_specs=[spec] * len(factors),
    )(*factors)


def owned_rows(left_side, right_side):
    blocks = lax.axis_size("blk")
    half = blocks // 2
    core = lax.axis_index("grp") % 2
    line = lax.axis_index("blk")
    width = left_side.shape[1] // 2
    sent = contract_rows(
        lax.dynamic_slice_in_dim(left_side, (1 - core) * width, width, 1), right_side
    ).astype(jnp.bfloat16)
    received = exchange(sent, "grp", 1)
    kept = contract_rows(lax.dynamic_slice_in_dim(left_side, core * width, width, 1), right_side)
    kept = kept + received.astype(jnp.float32)
    bit = half // 2
    while bit:
        width //= 2
        low = jnp.where(line & bit, width, 0)
        sent = lax.dynamic_slice_in_dim(kept, width - low, width, 0).astype(jnp.bfloat16)
        received = exchange(sent, "blk", bit)
        kept = lax.dynamic_slice_in_dim(kept, low, width, 0) + received.astype(jnp.float32)
        bit //= 2
    return relocate(kept.astype(jnp.bfloat16))


def owned_vector(values):
    blocks = lax.axis_size("blk")
    half = blocks // 2
    core = lax.axis_index("grp") % 2
    line = lax.axis_index("blk")
    kept = values.reshape(blocks, -1)
    count = half
    kept = lax.dynamic_slice_in_dim(kept, core * count, count, 0) + exchange(
        lax.dynamic_slice_in_dim(kept, (1 - core) * count, count, 0), "grp", 1
    )
    bit = half // 2
    while bit:
        count //= 2
        low = jnp.where(line & bit, count, 0)
        kept = lax.dynamic_slice_in_dim(kept, low, count, 0) + exchange(
            lax.dynamic_slice_in_dim(kept, count - low, count, 0), "blk", bit
        )
        bit //= 2
    return relocate(kept)[0]


def on_device(
    inputs,
    cotangent,
    master_attend,
    master_merge,
    master_expand,
    master_reduce,
    master_gains,
    moment_attend,
    moment_merge,
    moment_expand,
    moment_reduce,
    moment_gains,
    error_attend,
    error_merge,
    error_expand,
    error_reduce,
    start_attend,
    start_merge,
    start_expand,
    start_reduce,
):
    blocks = lax.axis_size("blk")
    groups = lax.axis_size("grp")
    group_index = lax.axis_index("grp")
    line_index = lax.axis_index("blk")
    half = blocks // 2
    block_index = group_index % 2 * half + line_index % half
    place = jnp.stack([group_index % 8, line_index]).astype(jnp.int32)
    prompt_size = SEG * blocks
    rows_low = relocate(inputs[0]).reshape(2 * SEG, D)
    gain_copy = lax.all_gather(master_gains, "blk", axis=0, tiled=True) if False else None
    gain_held = master_gains.astype(jnp.bfloat16)[None]
    for bit in bits_below(blocks):
        gain_held = jnp.concatenate([gain_held, exchange(gain_held, "blk", bit)])
    gain_copy = jnp.concatenate(
        [lax.dynamic_index_in_dim(gain_held, line_index ^ spot, 0, False) for spot in range(blocks)]
    )
    full_attend = gather_rows(master_attend.astype(jnp.bfloat16), 2, 2, place)
    full_merge = gather_rows(master_merge.astype(jnp.bfloat16), 8, 2, place)
    full_expand = gather_rows(master_expand.astype(jnp.bfloat16), 2, 4, place)
    full_reduce = gather_rows(master_reduce.astype(jnp.bfloat16), 8, 2, place)
    upstream = relocate(cotangent[0]).reshape(2 * SEG, D).astype(jnp.float32)
    gain_all = gain_copy.astype(jnp.float32)
    gain_first = gain_all[:D]
    gain_second = gain_all[D : 2 * D]
    gain_third = gain_all[2 * D : 3 * D]
    gain_fourth = gain_all[3 * D : 4 * D]
    gain_query = gain_all[4 * D : 4 * D + HD]
    gain_key = gain_all[4 * D + HD :]
    offsets = jnp.arange(SEG, dtype=jnp.int32)
    prompt_place = block_index * SEG + offsets
    reply_place = prompt_size + offsets
    cosine, sine_part = rope_tables(jnp.concatenate([prompt_place, reply_place]))
    rows_in = rows_low.astype(jnp.float32)
    normed_low = rmsnorm(rows_in, gain_first).astype(jnp.bfloat16)
    projected = jnp.dot(normed_low, full_attend, preferred_element_type=jnp.float32)
    query_rows, keys_rot, values_raw = prepare_heads(
        projected, gain_query, gain_key, cosine, sine_part
    )
    query_reduced = query_rows.astype(jnp.bfloat16).reshape(2, SEG, NH, HD)
    pair_low = jnp.concatenate([keys_rot, values_raw], axis=-1).astype(jnp.bfloat16)
    slots = pair_low[None, :SEG]
    for bit in bits_below(half):
        slots = jnp.concatenate([slots, exchange(slots, "blk", bit)])
    slots = jnp.concatenate([slots, exchange(slots, "grp", 1)])

    def prompt_pairs(wanted):
        return lax.dynamic_index_in_dim(slots, block_index ^ jnp.maximum(wanted, 0), 0, False)

    key_sets = jnp.stack(
        [
            jnp.concatenate(
                [prompt_pairs(block_index - 2), prompt_pairs(block_index - 1), pair_low[:SEG]]
            ),
            jnp.concatenate([prompt_pairs(blocks - 2), prompt_pairs(blocks - 1), pair_low[SEG:]]),
        ]
    )
    key_reduced = key_sets[..., :HD]
    value_reduced = key_sets[..., HD:]
    span = jnp.arange(WINDOW + SEG, dtype=jnp.int32)
    key_place = jnp.stack(
        [
            block_index * SEG - WINDOW + span,
            jnp.where(span < WINDOW, prompt_size - WINDOW + span, prompt_size + span - WINDOW),
        ]
    )
    query_place = jnp.stack([prompt_place, reply_place])
    distance = query_place[:, :, None] - key_place[:, None, :]
    allowed = (key_place[:, None, :] >= 0) & (distance >= 0) & (distance < WINDOW)

    def score_block():
        products = jnp.einsum(
            "itge,iue->igtu", query_reduced, key_reduced, preferred_element_type=jnp.float32
        )
        return jnp.where(allowed[:, None], products, NEG_FILL)

    attention_scores = score_block()
    top_score = jnp.max(attention_scores, axis=-1, keepdims=True)
    log_total = top_score + jnp.log(
        jnp.sum(jnp.exp(attention_scores - top_score), axis=-1, keepdims=True)
    )
    probability_reduced = jnp.exp(attention_scores - log_total).astype(jnp.bfloat16)
    attended = jnp.einsum(
        "ayco,aox->acyx", probability_reduced, value_reduced, preferred_element_type=jnp.float32
    )
    attended_low = attended.reshape(2 * SEG, HQ).astype(jnp.bfloat16)
    branch_attn = jnp.dot(attended_low, full_merge, preferred_element_type=jnp.float32)
    hidden = rows_in + rmsnorm(branch_attn, gain_second)
    normed_mid = rmsnorm(hidden, gain_third).astype(jnp.bfloat16)
    gate_up = jnp.dot(normed_mid, full_expand, preferred_element_type=jnp.float32)
    activated = gated_gelu(gate_up).astype(jnp.bfloat16)
    branch_ff = jnp.dot(activated, full_reduce, preferred_element_type=jnp.float32)
    result = hidden + rmsnorm(branch_ff, gain_fourth)
    block_output = relocate(result.astype(jnp.bfloat16)).reshape(1, 2, SEG, D)
    _, outer_back = jax.vjp(rmsnorm, branch_ff, gain_fourth)
    branch_grad, grad_fourth = outer_back(upstream)
    branch_low = branch_grad.astype(jnp.bfloat16)
    owned_reduce = owned_rows(activated, branch_low)
    active_grad = contract_cols(branch_low, full_reduce)
    _, gelu_back = jax.vjp(gated_gelu, gate_up)
    (expand_grad,) = gelu_back(active_grad)
    expand_low = expand_grad.astype(jnp.bfloat16)
    owned_expand = owned_rows(normed_mid, expand_low)
    middle_grad = contract_cols(expand_low, full_expand)
    _, third_back = jax.vjp(rmsnorm, hidden, gain_third)
    hidden_part, grad_third = third_back(middle_grad)
    hidden_grad = upstream + hidden_part
    _, second_back = jax.vjp(rmsnorm, branch_attn, gain_second)
    attn_grad, grad_second = second_back(hidden_grad)
    attn_low = attn_grad.astype(jnp.bfloat16)
    owned_merge = owned_rows(attended_low, attn_low)
    context_reduced = (
        contract_cols(attn_low, full_merge).astype(jnp.bfloat16).reshape(2, SEG, NH, HD)
    )
    attention_probabilities = jnp.exp(score_block() - log_total)
    probability_recomputed = attention_probabilities.astype(jnp.bfloat16)
    value_grad = jnp.einsum(
        "jsze,jzsf->jef",
        probability_recomputed,
        context_reduced,
        preferred_element_type=jnp.float32,
    )
    chance_grad = jnp.einsum(
        "itge,iue->igtu", context_reduced, value_reduced, preferred_element_type=jnp.float32
    )
    inner_sum = jnp.sum(attention_probabilities * chance_grad, axis=-1, keepdims=True)
    score_reduced = (attention_probabilities * (chance_grad - inner_sum)).astype(jnp.bfloat16)
    query_grad = jnp.einsum(
        "ayco,aox->acyx", score_reduced, key_reduced, preferred_element_type=jnp.float32
    )
    key_grad = jnp.einsum(
        "jsze,jzsf->jef", score_reduced, query_reduced, preferred_element_type=jnp.float32
    )
    pair_grad = jnp.concatenate([key_grad, value_grad], axis=-1)
    parts = pair_grad.reshape(2, WINDOW // SEG + 1, SEG, 2 * HD)
    kept = []
    for spot in range(blocks):
        target = block_index ^ spot
        total = parts[0, 2] if spot == 0 else jnp.zeros_like(parts[0, 2])
        for source, wanted in (
            (parts[0, 0], block_index - 2),
            (parts[0, 1], block_index - 1),
            (parts[1, 0], blocks - 2),
            (parts[1, 1], blocks - 1),
        ):
            total = total + jnp.where(target == wanted, source, 0.0)
        kept.append(total)
    kept = jnp.stack(kept)
    kept = kept[:half] + exchange(kept[half:].astype(jnp.bfloat16), "grp", 1).astype(jnp.float32)
    bit = half // 2
    while bit:
        kept = kept[:bit] + exchange(kept[bit:].astype(jnp.bfloat16), "blk", bit).astype(
            jnp.float32
        )
        bit //= 2
    pair_rows = jnp.concatenate([kept[0], parts[1, 2]], axis=0)

    def head_section(mixed_rows, query_gain, key_gain):
        return prepare_heads(mixed_rows, query_gain, key_gain, cosine, sine_part)

    _, heads_back = jax.vjp(head_section, projected, gain_query, gain_key)
    mixed_grad, grad_query, grad_key = heads_back(
        (query_grad.reshape(2 * SEG, NH, HD), pair_rows[:, :HD], pair_rows[:, HD:])
    )
    mixed_low = mixed_grad.astype(jnp.bfloat16)
    owned_attend = owned_rows(normed_low, mixed_low)
    normed_grad = contract_cols(mixed_low, full_attend)
    _, first_back = jax.vjp(rmsnorm, rows_in, gain_first)
    input_part, grad_first = first_back(normed_grad)
    input_grad = relocate((hidden_grad + input_part).astype(jnp.bfloat16))
    input_grad = input_grad.astype(jnp.float32).reshape(1, 2, SEG, D)
    owned_gains = owned_vector(
        jnp.concatenate([grad_first, grad_second, grad_third, grad_fourth, grad_query, grad_key])
    )
    owned_all = [
        owned.astype(jnp.float32) for owned in (owned_attend, owned_merge, owned_expand, owned_reduce)
    ]
    buffers = (error_attend, error_merge, error_expand, error_reduce)
    factors = (start_attend, start_merge, start_expand, start_reduce)
    combined = [owned + ERROR_KEEP * buffer[0] for owned, buffer in zip(owned_all, buffers)]

    def left_terms(members, extra):
        terms = [
            lax.dot_general(
                factors[member][0],
                combined[member],
                (((0,), (1,)), ((), ())),
                precision=lax.Precision.HIGHEST,
            )
            for member in members
        ]
        rank = terms[0].shape[0]
        flat = [term.reshape(-1) for term in terms] if False else terms
        joined = jnp.concatenate(flat + [part.reshape(rank, -1) for part in extra], axis=1)
        return sum_groups(joined)

    sums_late = left_terms((0, 1), (owned_gains,))
    sums_early = left_terms((2, 3), ())
    edge_early = combined[2].shape[0]
    edges_late = (combined[0].shape[0], combined[0].shape[0] + combined[1].shape[0])
    basis_early = orthonormal([sums_early[:, :edge_early], sums_early[:, edge_early:]])
    basis_late = orthonormal(
        [sums_late[:, : edges_late[0]], sums_late[:, edges_late[0] : edges_late[1]]]
    )
    gain_sums = sums_late[:, edges_late[1] :].reshape(-1)
    basis_set = [basis_late[0], basis_late[1], basis_early[0], basis_early[1]]
    rights = [
        jnp.dot(basis, matrix, precision=lax.Precision.HIGHEST)
        for matrix, basis in zip(combined, basis_set)
    ]
    residues = [
        matrix
        - lax.dot_general(
            basis, partial_right, (((0,), (0,)), ((), ())), precision=lax.Precision.HIGHEST
        )
        for matrix, basis, partial_right in zip(combined, basis_set, rights)
    ]

    def right_totals(members):
        joined = jnp.concatenate([rights[member] for member in members], axis=1)
        for bit in bits_below(groups):
            joined = joined + exchange(joined.astype(jnp.bfloat16), "grp", bit).astype(jnp.float32)
        return joined

    right_late = right_totals((0, 1))
    right_early = right_totals((2, 3))
    cut_late, cut_early = rights[0].shape[1], rights[2].shape[1]
    right_sums = [
        right_late[:, :cut_late],
        right_late[:, cut_late:],
        right_early[:, :cut_early],
        right_early[:, cut_early:],
    ]
    directions = [
        lax.dot_general(
            basis, summed, (((0,), (0,)), ((), ())), precision=lax.Precision.HIGHEST
        )
        / groups
        for basis, summed in zip(basis_set, right_sums)
    ]
    directions.append(gain_sums / groups)
    moments = (moment_attend, moment_merge, moment_expand, moment_reduce, moment_gains)
    masters = (master_attend, master_merge, master_expand, master_reduce, master_gains)
    velocities = [
        MOMENTUM * moment + (1.0 - MOMENTUM) * direction
        for moment, direction in zip(moments, directions)
    ]
    updated = [master - STEP_RATE * velocity for master, velocity in zip(masters, velocities)]
    return (
        (block_output, input_grad)
        + tuple(owned[None] for owned in owned_all)
        + (owned_gains[None],)
        + tuple(basis.T for basis in basis_set)
        + tuple(summed.T[None] for summed in right_sums)
        + tuple(residue[None] for residue in residues)
        + tuple(velocities)
        + tuple(updated)
        + tuple(weight.astype(jnp.bfloat16) for weight in updated)
    )


def solution(mesh):
    in_specs = (
        P("grp", None, "blk", None),
        P("grp", None, "blk", None),
        P("blk", None),
        P("blk", None),
        P("blk", None),
        P("blk", None),
        P("blk"),
        P("blk", None),
        P("blk", None),
        P("blk", None),
        P("blk", None),
        P("blk"),
        P("grp", "blk", None),
        P("grp", "blk", None),
        P("grp", "blk", None),
        P("grp", "blk", None),
        P("blk", None, None),
        P("blk", None, None),
        P("blk", None, None),
        P("blk", None, None),
    )
    out_specs = (
        P("grp", None, "blk", None),
        P("grp", None, "blk", None),
        P("grp", "blk", None),
        P("grp", "blk", None),
        P("grp", "blk", None),
        P("grp", "blk", None),
        P("grp", "blk"),
        P("blk", None),
        P("blk", None),
        P("blk", None),
        P("blk", None),
        P("blk", None, None),
        P("blk", None, None),
        P("blk", None, None),
        P("blk", None, None),
        P("grp", "blk", None),
        P("grp", "blk", None),
        P("grp", "blk", None),
        P("grp", "blk", None),
        P("blk", None),
        P("blk", None),
        P("blk", None),
        P("blk", None),
        P("blk"),
        P("blk", None),
        P("blk", None),
        P("blk", None),
        P("blk", None),
        P("blk"),
        P("blk", None),
        P("blk", None),
        P("blk", None),
        P("blk", None),
        P("blk"),
    )
    return jax.shard_map(
        on_device, mesh=mesh, in_specs=in_specs, out_specs=out_specs, check_vma=False
    )
```

```python
import jax
import jax.numpy as jnp
from jax import lax
from jax.experimental import pallas as pl
from jax.experimental.pallas import tpu as pltpu
from jax.sharding import PartitionSpec as P


D = 640
NH = 4
HD = 256
FF = 2048
WINDOW = 512
SEG = 256
HQ = 1024
QKV = 1536

NORM_EPS = 1e-06
ROPE_BASE = 10000.0
ERROR_KEEP = 0.5
MOMENTUM = 0.9
STEP_RATE = 0.02
NEG_FILL = -1e30
GELU_SCALE = 0.7978845608028654
GELU_CUBE = 0.044715

AXES = ("grp", "blk")
WHOLE = pl.BlockSpec(memory_space=pltpu.VMEM)
ANYWHERE = pl.BlockSpec(memory_space=pl.ANY)
SCALARS = pl.BlockSpec(memory_space=pltpu.SMEM)


def shape(dims, dtype):
    return jax.ShapeDtypeStruct(dims, dtype)


def rope_tables(places):
    frequency = jnp.arange(HD // 2, dtype=jnp.float32)
    inverse = ROPE_BASE ** (-2.0 * frequency / HD)
    angles = places.astype(jnp.float32)[:, None] * inverse[None, :]
    return (jnp.cos(angles), jnp.sin(angles))


def contract(left_side, right_side, left_axis, right_axis):
    return lax.dot_general(
        left_side,
        right_side,
        (((left_axis,), (right_axis,)), ((), ())),
        preferred_element_type=jnp.float32,
    )


def contract_rows(left_side, right_side):
    return contract(left_side, right_side, 0, 0)


def exchange(values, axis, bit):
    size = lax.axis_size(axis)
    return lax.ppermute(values, axis, [(place, place ^ bit) for place in range(size)])


def rising(limit):
    bit = 1
    while bit < limit:
        yield bit
        bit *= 2


def falling(limit):
    return list(rising(limit))[::-1]


def relocate(values):
    groups, blocks = lax.axis_size("grp"), lax.axis_size("blk")
    half = blocks // 2
    pairs = []
    for group in range(groups):
        for block in range(blocks):
            target = (group // 2 * 2 + block // half, group % 2 * half + block % half)
            if target != (group, block):
                pairs.append((group * blocks + block, target[0] * blocks + target[1]))
    moved = lax.ppermute(values, AXES, pairs)
    stays = lax.axis_index("grp") % 2 == lax.axis_index("blk") // half
    return jnp.where(stays, values, moved)


def sum_groups(values):
    for bit in rising(lax.axis_size("grp")):
        values = values + exchange(values, "grp", bit)
    return values


def line_masks(blocks):
    masks = [0]
    for bit in falling(blocks):
        masks += [mask ^ bit for mask in masks]
    return masks


def spread_line(mine):
    held = mine[None]
    for bit in falling(lax.axis_size("blk")):
        held = jnp.concatenate([held, exchange(held, "blk", bit)])
    return held


def spread_direct(held):
    held = held[None]
    held = jnp.concatenate([held] + [exchange(held, "grp", bit) for bit in (6, 2, 4)])
    return held, exchange(held, "grp", 1)


def spread_plane(held, first):
    held = held[None]
    held = jnp.concatenate([held, exchange(held, "grp", first)])
    held = jnp.concatenate([held, exchange(held, "grp", 6 - first)])
    return held, exchange(held, "grp", 1)


def piece_of(matrix, row_parts, part):
    height, width = matrix.shape
    if row_parts == 2:
        tall, wide = height // 2, width // 4
        start = ((part >> 2) * tall, (part & 3) * wide)
    else:
        tall, wide = height // 8, width
        start = (part * tall, 0)
    return lax.dynamic_slice(matrix, start, (tall, wide)).astype(jnp.bfloat16)


def weight_copies(place_ref, own, pieces, full, sems, row_parts, order, base):
    group, block = place_ref[0], place_ref[1]
    height, width = own.shape
    blocks = full.shape[0] // height
    tall, wide = (height // 2, width // 4) if row_parts == 2 else (height // 8, width)
    masks = line_masks(blocks)[1:]
    copies = [
        pltpu.make_async_copy(
            own, full.at[pl.ds(pl.multiple_of(block * height, height), height)], sems.at[0]
        )
    ]
    for side, held in enumerate(pieces):
        for spot, mask in enumerate(order):
            part = lax.bitwise_xor(group, mask + side)
            row_part, column_part = (part >> 2, part & 3) if row_parts == 2 else (part, 0)
            for step, line_mask in enumerate(masks):
                start = lax.bitwise_xor(block, line_mask) * height + row_part * tall
                target = full.at[
                    pl.ds(pl.multiple_of(start, tall), tall),
                    pl.ds(pl.multiple_of(column_part * wide, wide), wide),
                ]
                source = held.at[spot, step, pl.ds(base, tall), pl.ds(0, wide)]
                copies.append(pltpu.make_async_copy(source, target, sems.at[len(copies)]))
    return copies


def inverse_rms(values):
    return lax.rsqrt(jnp.mean(values * values, axis=-1, keepdims=True) + NORM_EPS)


def norm_back(values, scale, gain, upstream):
    lifted = (1.0 + gain) * upstream
    inner = jnp.mean(values * lifted, axis=-1, keepdims=True)
    gain_part = jnp.sum(values * scale * upstream, axis=0, keepdims=True)
    return scale * lifted - values * (scale * scale * scale * inner), gain_part


def turn(values, cosine, sine):
    middle = HD // 2
    low, high = values[:, :middle], values[:, middle:]
    return jnp.concatenate([low * cosine - high * sine, high * cosine + low * sine], axis=1)


def turn_back(values, cosine, sine):
    middle = HD // 2
    low, high = values[:, :middle], values[:, middle:]
    return jnp.concatenate([low * cosine + high * sine, high * cosine - low * sine], axis=1)


def pairs_kernel(
    place_ref, rows_ref, gain_ref, head_gain_ref, cos_ref, sin_ref, own, near, far,
    full_ref, normed_ref, raw_ref, pair_ref, sems,
):
    copies = weight_copies(place_ref, own, (near, far), full_ref, sems, 2, (0, 6, 2, 4), 0)
    for copy in copies:
        copy.start()
    rows = rows_ref[...].astype(jnp.float32)
    normed = (rows * inverse_rms(rows) * (1.0 + gain_ref[0:1])).astype(jnp.bfloat16)
    normed_ref[...] = normed
    for copy in copies:
        copy.wait()
    raw = jnp.dot(normed, full_ref[:, HQ:], preferred_element_type=jnp.float32)
    raw_ref[...] = raw
    keys = raw[:, :HD]
    keys = turn(keys * inverse_rms(keys) * (1.0 + head_gain_ref[1:2]), cos_ref[...], sin_ref[...])
    pair_ref[...] = jnp.concatenate([keys, raw[:, HD:]], axis=1).astype(jnp.bfloat16)


def queries_kernel(normed_ref, full_ref, head_gain_ref, cos_ref, sin_ref, raw_ref, query_ref):
    for head in range(NH):
        columns = slice(head * HD, (head + 1) * HD)
        raw = jnp.dot(normed_ref[...], full_ref[:, columns], preferred_element_type=jnp.float32)
        raw_ref[:, columns] = raw
        query = raw * inverse_rms(raw) * (1.0 + head_gain_ref[0:1])
        query = turn(query, cos_ref[...], sin_ref[...]) * HD ** (-0.5)
        query_ref[0, head] = query[:SEG].astype(jnp.bfloat16)
        query_ref[1, head] = query[SEG:].astype(jnp.bfloat16)


def attend_kernel(spots_ref, query_ref, far_ref, mid_ref, own_ref, chance_ref, context_ref):
    part = pl.program_id(0)
    rows = lax.broadcasted_iota(jnp.int32, (SEG, SEG), 0)
    columns = lax.broadcasted_iota(jnp.int32, (SEG, SEG), 1)
    far_open = (rows < columns) & (spots_ref[4 + 2 * part] > 0)
    mid_open = (rows >= 0) & (spots_ref[5 + 2 * part] > 0)
    own_open = rows >= columns
    for head in range(NH):
        query = query_ref[0, head]
        scores = jnp.concatenate(
            [
                jnp.where(open_, contract(query, ref[0, :, :HD], 1, 1), NEG_FILL)
                for ref, open_ in ((far_ref, far_open), (mid_ref, mid_open), (own_ref, own_open))
            ],
            axis=1,
        )
        chance = jnp.exp(scores - jnp.max(scores, axis=1, keepdims=True))
        chance = (chance / jnp.sum(chance, axis=1, keepdims=True)).astype(jnp.bfloat16)
        chance_ref[0, head] = chance
        context = jnp.dot(chance[:, :SEG], far_ref[0, :, HD:], preferred_element_type=jnp.float32)
        context += jnp.dot(
            chance[:, SEG : 2 * SEG], mid_ref[0, :, HD:], preferred_element_type=jnp.float32
        )
        context += jnp.dot(
            chance[:, 2 * SEG :], own_ref[0, :, HD:], preferred_element_type=jnp.float32
        )
        context_ref[:, head * HD : (head + 1) * HD] = context.astype(jnp.bfloat16)


TILE = 512


def start_and_arrive(step, groups):
    @pl.when(step == 0)
    def _():
        for copies in groups:
            for copy in copies():
                copy.start()

    def arrive(which):
        @pl.when(step == 0)
        def _():
            for copy in groups[which]():
                copy.wait()

    return arrive


def front_kernel(
    place_ref, rows_ref, context_ref, upstream_ref, gain_ref, own_merge, own_expand, own_reduce,
    even_a, even_b, odd_a, odd_b,
    output_ref, hidden_ref, merged_ref, normed_ref, active_ref, gated_ref, lifted_ref, branch_ref,
    gain_grad_ref,
    merge, expand, reduce, sems_merge, sems_expand, sems_reduce,
):
    step = pl.program_id(0)
    even, odd = (even_a, even_b), (odd_a, odd_b)
    base = own_merge.shape[0] // 8
    arrive = start_and_arrive(
        step,
        (
            lambda: weight_copies(place_ref, own_merge, even, merge, sems_merge, 8, (0, 2, 4, 6), 0),
            lambda: weight_copies(place_ref, own_expand, odd, expand, sems_expand, 2, (0, 4, 2, 6), 0),
            lambda: weight_copies(place_ref, own_reduce, even, reduce, sems_reduce, 8, (0, 2, 4, 6), base),
        ),
    )

    @pl.when(step == 0)
    def _():
        gain_grad_ref[...] = jnp.zeros_like(gain_grad_ref)

    second, third, fourth = gain_ref[1:2], gain_ref[2:3], gain_ref[3:4]
    arrive(0)
    branch = jnp.dot(context_ref[...], merge[...], preferred_element_type=jnp.float32)
    merged_ref[...] = branch
    hidden = rows_ref[...].astype(jnp.float32) + branch * inverse_rms(branch) * (1.0 + second)
    hidden_ref[...] = hidden
    normed_ref[...] = (hidden * inverse_rms(hidden) * (1.0 + third)).astype(jnp.bfloat16)
    arrive(1)

    def forward(tile, carry):
        low = pl.ds(pl.multiple_of(tile * TILE, TILE), TILE)
        high = pl.ds(pl.multiple_of(FF + tile * TILE, TILE), TILE)
        gate = jnp.dot(normed_ref[...], expand[:, low], preferred_element_type=jnp.float32)
        up = jnp.dot(normed_ref[...], expand[:, high], preferred_element_type=jnp.float32)
        square = gate * gate
        bend = jnp.tanh(GELU_SCALE * gate * (1.0 + GELU_CUBE * square))
        share = 0.5 * (1.0 + bend)
        gelu = gate * share
        slope = share + gelu * (1.0 - bend) * (
            GELU_SCALE + (3.0 * GELU_CUBE * GELU_SCALE) * square
        )
        gated_ref[:, low] = gelu.astype(jnp.bfloat16)
        lifted_ref[:, low] = (up * slope).astype(jnp.bfloat16)
        active_ref[:, low] = (gelu * up).astype(jnp.bfloat16)
        return carry

    lax.fori_loop(0, FF // TILE, forward, 0)
    arrive(2)
    outer = jnp.dot(active_ref[...], reduce[...], preferred_element_type=jnp.float32)
    outer_scale = inverse_rms(outer)
    output_ref[...] = (hidden + outer * outer_scale * (1.0 + fourth)).astype(jnp.bfloat16)
    upstream = upstream_ref[...].astype(jnp.float32)
    outer_grad, fourth_part = norm_back(outer, outer_scale, fourth, upstream)
    branch_ref[...] = outer_grad.astype(jnp.bfloat16)
    gain_grad_ref[0:1] += fourth_part


def back_kernel(
    place_ref, branch_ref, gated_ref, lifted_ref, upstream_ref, hidden_ref, merged_ref, gain_ref,
    own_merge, own_expand, own_reduce,
    even_a, even_b, odd_a, odd_b,
    expand_ref, hidden_grad_ref, attn_ref, context_ref, gain_grad_ref,
    merge, expand, reduce, sems_merge, sems_expand, sems_reduce,
):
    step = pl.program_id(0)
    even, odd = (even_a, even_b), (odd_a, odd_b)
    base = own_merge.shape[0] // 8
    arrive = start_and_arrive(
        step,
        (
            lambda: weight_copies(place_ref, own_reduce, even, reduce, sems_reduce, 8, (0, 2, 4, 6), base),
            lambda: weight_copies(place_ref, own_expand, odd, expand, sems_expand, 2, (0, 4, 2, 6), 0),
            lambda: weight_copies(place_ref, own_merge, even, merge, sems_merge, 8, (0, 2, 4, 6), 0),
        ),
    )

    @pl.when(step == 0)
    def _():
        gain_grad_ref[...] = jnp.zeros_like(gain_grad_ref)

    second, third = gain_ref[1:2], gain_ref[2:3]
    arrive(0)

    def backward(tile, carry):
        low = pl.ds(pl.multiple_of(tile * TILE, TILE), TILE)
        high = pl.ds(pl.multiple_of(FF + tile * TILE, TILE), TILE)
        grad = contract(branch_ref[...], reduce[low, :], 1, 1)
        expand_ref[:, low] = (grad * lifted_ref[:, low].astype(jnp.float32)).astype(jnp.bfloat16)
        expand_ref[:, high] = (grad * gated_ref[:, low].astype(jnp.float32)).astype(jnp.bfloat16)
        return carry

    lax.fori_loop(0, FF // TILE, backward, 0)
    arrive(1)
    middle_grad = contract(expand_ref[...], expand[...], 1, 1)
    hidden, branch = hidden_ref[...], merged_ref[...]
    hidden_part, third_part = norm_back(hidden, inverse_rms(hidden), third, middle_grad)
    hidden_grad = upstream_ref[...].astype(jnp.float32) + hidden_part
    hidden_grad_ref[...] = hidden_grad
    attn_grad, second_part = norm_back(branch, inverse_rms(branch), second, hidden_grad)
    attn_ref[...] = attn_grad.astype(jnp.bfloat16)
    gain_grad_ref[0:1] += second_part
    gain_grad_ref[1:2] += third_part
    arrive(2)
    for head in range(NH):
        context_ref[0, head] = contract(
            attn_ref[...], merge[head * HD : (head + 1) * HD, :], 1, 1
        ).astype(jnp.bfloat16)


def attend_back_kernel(
    spots_ref, query_ref, far_ref, mid_ref, own_ref, chance_ref, context_ref, raw_ref,
    head_gain_ref, cos_ref, sin_ref,
    mixed_ref, kept_ref, sent_ref, reply_ref, gain_grad_ref,
    total, score_low,
):
    part = pl.program_id(0)

    @pl.when(part == 0)
    def _():
        total[...] = jnp.zeros_like(total)
        gain_grad_ref[...] = jnp.zeros_like(gain_grad_ref)

    gain = head_gain_ref[0:1]
    for head in range(NH):
        context = context_ref[0, head]
        grad = jnp.concatenate(
            [contract(context, ref[0, :, HD:], 1, 1) for ref in (far_ref, mid_ref, own_ref)], axis=1
        )
        chance = chance_ref[0, head].astype(jnp.float32)
        inner = jnp.sum(chance * grad, axis=1, keepdims=True)
        score = (chance * (grad - inner)).astype(jnp.bfloat16)
        score_low[head * SEG : (head + 1) * SEG, :] = score
        query_grad = jnp.dot(score[:, :SEG], far_ref[0, :, :HD], preferred_element_type=jnp.float32)
        query_grad += jnp.dot(
            score[:, SEG : 2 * SEG], mid_ref[0, :, :HD], preferred_element_type=jnp.float32
        )
        query_grad += jnp.dot(
            score[:, 2 * SEG :], own_ref[0, :, :HD], preferred_element_type=jnp.float32
        )
        turned = turn_back(query_grad * HD ** (-0.5), cos_ref[...], sin_ref[...])
        columns = slice(head * HD, (head + 1) * HD)
        raw = raw_ref[:, columns]
        mixed, gain_part = norm_back(raw, inverse_rms(raw), gain, turned)
        mixed_ref[:, columns] = mixed.astype(jnp.bfloat16)
        gain_grad_ref[0:1] += gain_part
    queries = query_ref[0].reshape(NH * SEG, HD)
    contexts = context_ref[0].reshape(NH * SEG, HD)
    chances = chance_ref[0].reshape(NH * SEG, WINDOW + SEG)
    for spot in range(3):
        columns = slice(spot * SEG, (spot + 1) * SEG)
        key_grad = contract(score_low[:, columns], queries, 0, 0)
        value_grad = contract(chances[:, columns], contexts, 0, 0)
        if spot < 2:
            slot = spots_ref[2 * part + spot]
            total[slot, :, :HD] += key_grad
            total[slot, :, HD:] += value_grad
        else:

            @pl.when(part == 0)
            def _():
                total[0, :, :HD] += key_grad
                total[0, :, HD:] += value_grad

            @pl.when(part == 1)
            def _():
                reply_ref[:, :HD] = key_grad
                reply_ref[:, HD:] = value_grad

    @pl.when(part == 1)
    def _():
        half = total.shape[0] // 2
        kept_ref[...] = total[:half]
        sent_ref[...] = total[half:].astype(jnp.bfloat16)


def inputs_back_kernel(
    rows_ref, mixed_ref, pair_grad_ref, raw_ref, full_ref, hidden_grad_ref, gain_ref,
    head_gain_ref, cos_ref, sin_ref,
    low_ref, input_grad_ref, gain_grad_ref, key_grad_ref,
):
    @pl.when(pl.program_id(0) == 0)
    def _():
        gain_grad_ref[...] = jnp.zeros_like(gain_grad_ref)
        key_grad_ref[...] = jnp.zeros_like(key_grad_ref)

    keys = raw_ref[:, :HD]
    turned = turn_back(pair_grad_ref[0, :, :HD], cos_ref[...], sin_ref[...])
    key_part, key_gain = norm_back(keys, inverse_rms(keys), head_gain_ref[1:2], turned)
    low_ref[:, :HQ] = mixed_ref[...]
    low_ref[:, HQ : HQ + HD] = key_part.astype(jnp.bfloat16)
    low_ref[:, HQ + HD :] = pair_grad_ref[0, :, HD:].astype(jnp.bfloat16)
    normed_grad = contract(low_ref[...], full_ref[...], 1, 1)
    rows = rows_ref[...].astype(jnp.float32)
    input_part, first_part = norm_back(rows, inverse_rms(rows), gain_ref[0:1], normed_grad)
    input_grad_ref[...] = (hidden_grad_ref[...] + input_part).astype(jnp.bfloat16)
    gain_grad_ref[0:1] += first_part
    key_grad_ref[0:1] += key_gain


def orthonormal_kernel(*refs):
    count = len(refs) // 2
    factors = [ref[...] for ref in refs[:count]]
    rows = lax.broadcasted_iota(jnp.int32, (factors[0].shape[0], 1), 0)
    for column in range(factors[0].shape[0]):
        for member in range(count):
            factor = factors[member]
            vector = factor[column : column + 1]
            inner = jnp.sum(factor * vector, axis=1, keepdims=True)
            scale = lax.rsqrt(inner[column : column + 1] + NORM_EPS)
            basis = vector * scale
            weights = jnp.where(rows > column, inner * scale, 0.0)
            factors[member] = jnp.where(rows == column, basis, factor - weights * basis)
    for member in range(count):
        refs[count + member][...] = factors[member]


def orthonormal(factors):
    return pl.pallas_call(
        orthonormal_kernel,
        out_shape=[shape(factor.shape, factor.dtype) for factor in factors],
        in_specs=[WHOLE] * len(factors),
        out_specs=[WHOLE] * len(factors),
    )(*factors)


def owned_rows(left_side, right_side):
    blocks = lax.axis_size("blk")
    half = blocks // 2
    core = lax.axis_index("grp") % 2
    line = lax.axis_index("blk")
    width = left_side.shape[1] // 2
    sent = contract_rows(
        lax.dynamic_slice_in_dim(left_side, (1 - core) * width, width, 1), right_side
    ).astype(jnp.bfloat16)
    received = exchange(sent, "grp", 1)
    kept = contract_rows(lax.dynamic_slice_in_dim(left_side, core * width, width, 1), right_side)
    kept = kept + received.astype(jnp.float32)
    bit = half // 2
    while bit:
        width //= 2
        low = jnp.where(line & bit, width, 0)
        sent = lax.dynamic_slice_in_dim(kept, width - low, width, 0).astype(jnp.bfloat16)
        received = exchange(sent, "blk", bit)
        kept = lax.dynamic_slice_in_dim(kept, low, width, 0) + received.astype(jnp.float32)
        bit //= 2
    return relocate(kept.astype(jnp.bfloat16))


def owned_vector(values):
    blocks = lax.axis_size("blk")
    half = blocks // 2
    core = lax.axis_index("grp") % 2
    line = lax.axis_index("blk")
    kept = values.reshape(blocks, -1)
    count = half
    kept = lax.dynamic_slice_in_dim(kept, core * count, count, 0) + exchange(
        lax.dynamic_slice_in_dim(kept, (1 - core) * count, count, 0), "grp", 1
    )
    bit = half // 2
    while bit:
        count //= 2
        low = jnp.where(line & bit, count, 0)
        kept = lax.dynamic_slice_in_dim(kept, low, count, 0) + exchange(
            lax.dynamic_slice_in_dim(kept, count - low, count, 0), "blk", bit
        )
        bit //= 2
    return relocate(kept)[0]


def on_device(
    inputs,
    cotangent,
    master_attend,
    master_merge,
    master_expand,
    master_reduce,
    master_gains,
    moment_attend,
    moment_merge,
    moment_expand,
    moment_reduce,
    moment_gains,
    error_attend,
    error_merge,
    error_expand,
    error_reduce,
    start_attend,
    start_merge,
    start_expand,
    start_reduce,
):
    blocks = lax.axis_size("blk")
    groups = lax.axis_size("grp")
    group_index = lax.axis_index("grp")
    line_index = lax.axis_index("blk")
    half = blocks // 2
    tokens = 2 * SEG
    block_index = group_index % 2 * half + line_index % half
    part = group_index % 8
    place = jnp.stack([part, line_index]).astype(jnp.int32)
    prompt_size = SEG * blocks

    attend_piece = jnp.concatenate(
        [piece_of(master_attend, 2, part), master_gains.astype(jnp.bfloat16).reshape(-1, QKV // 4)]
    )
    tall_attend = master_attend.shape[0] // 2
    held_attend = spread_line(attend_piece)
    rows_low = relocate(inputs[0]).reshape(tokens, D)
    even_piece = jnp.concatenate(
        [piece_of(master_merge, 8, part), piece_of(master_reduce, 8, part)]
    )
    near_attend, far_attend = spread_direct(held_attend[1:])
    even_pieces = spread_plane(spread_line(even_piece)[1:], 2)
    odd_pieces = spread_plane(spread_line(piece_of(master_expand, 2, part))[1:], 4)
    upstream_low = relocate(cotangent[0]).reshape(tokens, D)
    masks = line_masks(blocks)
    gain_slots = held_attend[:, tall_attend:].reshape(blocks, -1)
    gain_slots = jnp.stack([gain_slots[masks.index(spot)] for spot in range(blocks)])
    gain_copy = jnp.concatenate(
        [lax.dynamic_index_in_dim(gain_slots, line_index ^ spot, 0, False) for spot in range(blocks)]
    )
    gain_all = gain_copy.astype(jnp.float32)
    gain_wide = gain_all[: 4 * D].reshape(4, D)
    gain_head = gain_all[4 * D :].reshape(2, HD)
    offsets = jnp.arange(SEG, dtype=jnp.int32)
    cosine, sine = rope_tables(
        jnp.concatenate([block_index * SEG + offsets, prompt_size + offsets])
    )

    full_attend, normed_low, raw_pairs, pair_low = pl.pallas_call(
        pairs_kernel,
        out_shape=[
            shape((D, QKV), jnp.bfloat16),
            shape((tokens, D), jnp.bfloat16),
            shape((tokens, 2 * HD), jnp.float32),
            shape((tokens, 2 * HD), jnp.bfloat16),
        ],
        in_specs=[SCALARS] + [WHOLE] * 5 + [ANYWHERE] * 3,
        out_specs=[WHOLE] * 4,
        scratch_shapes=[pltpu.SemaphoreType.DMA((1 + 8 * (blocks - 1),))],
        cost_estimate=pl.CostEstimate(flops=6 * 10**8, bytes_accessed=9 * 10**6, transcendentals=0),
    )(
        place, rows_low, gain_wide, gain_head, cosine, sine,
        master_attend.astype(jnp.bfloat16), near_attend, far_attend,
    )
    slots = pair_low[None, :SEG]
    for bit in rising(half):
        slots = jnp.concatenate([slots, exchange(slots, "blk", bit)])
    slots = jnp.concatenate([slots, exchange(slots, "grp", 1)])
    raw_queries, queries = pl.pallas_call(
        queries_kernel,
        out_shape=[
            shape((tokens, HQ), jnp.float32),
            shape((2, NH, SEG, HD), jnp.bfloat16),
        ],
        in_specs=[WHOLE] * 5,
        out_specs=[WHOLE] * 2,
        cost_estimate=pl.CostEstimate(flops=12 * 10**8, bytes_accessed=9 * 10**6, transcendentals=0),
    )(normed_low, full_attend, gain_head, cosine, sine)

    wanted = jnp.stack([block_index - 2, block_index - 1, blocks - 2 + 0 * part, blocks - 1 + 0 * part])
    spots = jnp.concatenate([block_index ^ jnp.maximum(wanted, 0), wanted >= 0]).astype(jnp.int32)
    own_pairs = pair_low.reshape(2, SEG, 2 * HD)
    slot_specs = [
        pl.BlockSpec((1, SEG, 2 * HD), lambda i, s: (s[2 * i], 0, 0)),
        pl.BlockSpec((1, SEG, 2 * HD), lambda i, s: (s[2 * i + 1], 0, 0)),
        pl.BlockSpec((1, SEG, 2 * HD), lambda i, s: (i, 0, 0)),
    ]
    head_spec = pl.BlockSpec((1, NH, SEG, HD), lambda i, s: (i, 0, 0, 0))
    chance_spec = pl.BlockSpec((1, NH, SEG, WINDOW + SEG), lambda i, s: (i, 0, 0, 0))
    rows_spec = pl.BlockSpec((SEG, HQ), lambda i, s: (i, 0))
    chances, context_low = pl.pallas_call(
        attend_kernel,
        out_shape=[
            shape((2, NH, SEG, WINDOW + SEG), jnp.bfloat16),
            shape((tokens, HQ), jnp.bfloat16),
        ],
        grid_spec=pltpu.PrefetchScalarGridSpec(
            num_scalar_prefetch=1,
            grid=(2,),
            in_specs=[head_spec] + slot_specs,
            out_specs=[chance_spec, rows_spec],
        ),
        cost_estimate=pl.CostEstimate(flops=17 * 10**8, bytes_accessed=9 * 10**6, transcendentals=1600000),
    )(spots, queries, slots, slots, own_pairs)

    chunk = lambda width: pl.BlockSpec((SEG, width), lambda i: (i, 0))
    fixed = lambda rows, width: pl.BlockSpec((rows, width), lambda i: (0, 0))
    sem_count = 1 + 8 * (blocks - 1)
    weight_specs = [ANYWHERE] * 7
    weight_args = (
        master_merge.astype(jnp.bfloat16), master_expand.astype(jnp.bfloat16),
        master_reduce.astype(jnp.bfloat16), *even_pieces, *odd_pieces,
    )
    weight_scratch = [
        pltpu.VMEM((HQ, D), jnp.bfloat16),
        pltpu.VMEM((D, 2 * FF), jnp.bfloat16),
        pltpu.VMEM((FF, D), jnp.bfloat16),
    ] + [pltpu.SemaphoreType.DMA((sem_count,))] * 3
    (
        output_low, hidden, merged, normed_mid, activated, gated, lifted, branch_low,
        fourth_grads,
    ) = pl.pallas_call(
        front_kernel,
        out_shape=[
            shape((tokens, D), jnp.bfloat16),
            shape((tokens, D), jnp.float32),
            shape((tokens, D), jnp.float32),
            shape((tokens, D), jnp.bfloat16),
            shape((tokens, FF), jnp.bfloat16),
            shape((tokens, FF), jnp.bfloat16),
            shape((tokens, FF), jnp.bfloat16),
            shape((tokens, D), jnp.bfloat16),
            shape((8, D), jnp.float32),
        ],
        grid=(2,),
        in_specs=[SCALARS, chunk(D), chunk(HQ), chunk(D), fixed(4, D)] + weight_specs,
        out_specs=[
            chunk(D), chunk(D), chunk(D), chunk(D), chunk(FF), chunk(FF), chunk(FF), chunk(D),
            fixed(8, D),
        ],
        scratch_shapes=weight_scratch,
        cost_estimate=pl.CostEstimate(
            flops=47 * 10**8, bytes_accessed=20 * 10**6, transcendentals=10**6
        ),
    )(place, rows_low, context_low, upstream_low, gain_wide, *weight_args)
    owned_reduce = owned_rows(activated, branch_low)
    expand_low, hidden_grad, attn_low, context_grad, wide_grads = pl.pallas_call(
        back_kernel,
        out_shape=[
            shape((tokens, 2 * FF), jnp.bfloat16),
            shape((tokens, D), jnp.float32),
            shape((tokens, D), jnp.bfloat16),
            shape((2, NH, SEG, HD), jnp.bfloat16),
            shape((8, D), jnp.float32),
        ],
        grid=(2,),
        in_specs=[
            SCALARS, chunk(D), chunk(FF), chunk(FF), chunk(D), chunk(D), chunk(D), fixed(4, D),
        ]
        + weight_specs,
        out_specs=[
            chunk(2 * FF), chunk(D), chunk(D),
            pl.BlockSpec((1, NH, SEG, HD), lambda i: (i, 0, 0, 0)), fixed(8, D),
        ],
        scratch_shapes=weight_scratch,
        cost_estimate=pl.CostEstimate(
            flops=47 * 10**8, bytes_accessed=20 * 10**6, transcendentals=0
        ),
    )(
        place, branch_low, gated, lifted, upstream_low, hidden, merged, gain_wide, *weight_args
    )
    owned_gate = owned_rows(normed_mid, expand_low[:, :FF])
    owned_up = owned_rows(normed_mid, expand_low[:, FF:])
    owned_merge = owned_rows(context_low, attn_low)
    owned_expand = jnp.concatenate([owned_gate, owned_up], axis=1)

    mixed_queries, kept, sent, reply, query_gain = pl.pallas_call(
        attend_back_kernel,
        out_shape=[
            shape((tokens, HQ), jnp.bfloat16),
            shape((half, SEG, 2 * HD), jnp.float32),
            shape((half, SEG, 2 * HD), jnp.bfloat16),
            shape((SEG, 2 * HD), jnp.float32),
            shape((8, HD), jnp.float32),
        ],
        grid_spec=pltpu.PrefetchScalarGridSpec(
            num_scalar_prefetch=1,
            grid=(2,),
            in_specs=[head_spec]
            + slot_specs
            + [
                chance_spec,
                head_spec,
                rows_spec,
                pl.BlockSpec((2, HD), lambda i, s: (0, 0)),
                pl.BlockSpec((SEG, HD // 2), lambda i, s: (i, 0)),
                pl.BlockSpec((SEG, HD // 2), lambda i, s: (i, 0)),
            ],
            out_specs=[
                rows_spec,
                pl.BlockSpec((half, SEG, 2 * HD), lambda i, s: (0, 0, 0)),
                pl.BlockSpec((half, SEG, 2 * HD), lambda i, s: (0, 0, 0)),
                pl.BlockSpec((SEG, 2 * HD), lambda i, s: (0, 0)),
                pl.BlockSpec((8, HD), lambda i, s: (0, 0)),
            ],
            scratch_shapes=[
                pltpu.VMEM((blocks, SEG, 2 * HD), jnp.float32),
                pltpu.VMEM((NH * SEG, WINDOW + SEG), jnp.bfloat16),
            ],
        ),
        cost_estimate=pl.CostEstimate(flops=35 * 10**8, bytes_accessed=15 * 10**6, transcendentals=0),
    )(
        spots, queries, slots, slots, own_pairs, chances, context_grad, raw_queries, gain_head,
        cosine, sine,
    )
    kept = kept + exchange(sent, "grp", 1).astype(jnp.float32)
    for bit in falling(half):
        kept = kept[:bit] + exchange(kept[bit:].astype(jnp.bfloat16), "blk", bit).astype(
            jnp.float32
        )
    pair_grads = jnp.concatenate([kept, reply[None]])
    mixed_low, input_low, first_grads, key_gain = pl.pallas_call(
        inputs_back_kernel,
        out_shape=[
            shape((tokens, QKV), jnp.bfloat16),
            shape((tokens, D), jnp.bfloat16),
            shape((8, D), jnp.float32),
            shape((8, HD), jnp.float32),
        ],
        grid=(2,),
        in_specs=[
            chunk(D), chunk(HQ), pl.BlockSpec((1, SEG, 2 * HD), lambda i: (i, 0, 0)),
            chunk(2 * HD), fixed(D, QKV), chunk(D), fixed(4, D), fixed(2, HD), chunk(HD // 2),
            chunk(HD // 2),
        ],
        out_specs=[chunk(QKV), chunk(D), fixed(8, D), fixed(8, HD)],
        cost_estimate=pl.CostEstimate(flops=12 * 10**8, bytes_accessed=9 * 10**6, transcendentals=0),
    )(
        rows_low, mixed_queries, pair_grads, raw_pairs, full_attend, hidden_grad, gain_wide,
        gain_head, cosine, sine,
    )
    owned_attend = owned_rows(normed_low, mixed_low)
    input_grad = relocate(input_low).astype(jnp.float32).reshape(1, 2, SEG, D)
    owned_gains = owned_vector(
        jnp.concatenate(
            [
                first_grads[0], wide_grads[0], wide_grads[1], fourth_grads[0], query_gain[0],
                key_gain[0],
            ]
        ),
    )
    block_output = relocate(output_low).reshape(1, 2, SEG, D)

    owned_all = [
        owned.astype(jnp.float32) for owned in (owned_attend, owned_merge, owned_expand, owned_reduce)
    ]
    buffers = (error_attend, error_merge, error_expand, error_reduce)
    factors = (start_attend, start_merge, start_expand, start_reduce)
    combined = [owned + ERROR_KEEP * buffer[0] for owned, buffer in zip(owned_all, buffers)]

    def left_terms(members, extra):
        terms = [
            lax.dot_general(
                factors[member][0],
                combined[member],
                (((0,), (1,)), ((), ())),
                precision=lax.Precision.HIGHEST,
            )
            for member in members
        ]
        rank = terms[0].shape[0]
        joined = jnp.concatenate(terms + [part.reshape(rank, -1) for part in extra], axis=1)
        return sum_groups(joined)

    sums_late = left_terms((0, 1), (owned_gains,))
    sums_early = left_terms((2, 3), ())
    edge_early = combined[2].shape[0]
    edges_late = (combined[0].shape[0], combined[0].shape[0] + combined[1].shape[0])
    basis_early = orthonormal([sums_early[:, :edge_early], sums_early[:, edge_early:]])
    basis_late = orthonormal(
        [sums_late[:, : edges_late[0]], sums_late[:, edges_late[0] : edges_late[1]]]
    )
    gain_sums = sums_late[:, edges_late[1] :].reshape(-1)
    basis_set = [basis_late[0], basis_late[1], basis_early[0], basis_early[1]]
    rights = [
        jnp.dot(basis, matrix, precision=lax.Precision.HIGHEST)
        for matrix, basis in zip(combined, basis_set)
    ]
    residues = [
        matrix
        - lax.dot_general(
            basis, partial_right, (((0,), (0,)), ((), ())), precision=lax.Precision.HIGHEST
        )
        for matrix, basis, partial_right in zip(combined, basis_set, rights)
    ]

    def right_totals(members):
        joined = jnp.concatenate([rights[member] for member in members], axis=1)
        for bit in rising(groups):
            joined = joined + exchange(joined.astype(jnp.bfloat16), "grp", bit).astype(jnp.float32)
        return joined

    right_late = right_totals((0, 1))
    right_early = right_totals((2, 3))
    cut_late, cut_early = rights[0].shape[1], rights[2].shape[1]
    right_sums = [
        right_late[:, :cut_late],
        right_late[:, cut_late:],
        right_early[:, :cut_early],
        right_early[:, cut_early:],
    ]
    directions = [
        lax.dot_general(
            basis, summed, (((0,), (0,)), ((), ())), precision=lax.Precision.HIGHEST
        )
        / groups
        for basis, summed in zip(basis_set, right_sums)
    ]
    directions.append(gain_sums / groups)
    moments = (moment_attend, moment_merge, moment_expand, moment_reduce, moment_gains)
    masters = (master_attend, master_merge, master_expand, master_reduce, master_gains)
    velocities = [
        MOMENTUM * moment + (1.0 - MOMENTUM) * direction
        for moment, direction in zip(moments, directions)
    ]
    updated = [master - STEP_RATE * velocity for master, velocity in zip(masters, velocities)]
    return (
        (block_output, input_grad)
        + tuple(owned[None] for owned in owned_all)
        + (owned_gains[None],)
        + tuple(basis.T for basis in basis_set)
        + tuple(summed.T[None] for summed in right_sums)
        + tuple(residue[None] for residue in residues)
        + tuple(velocities)
        + tuple(updated)
        + tuple(weight.astype(jnp.bfloat16) for weight in updated)
    )


def solution(mesh):
    in_specs = (
        P("grp", None, "blk", None),
        P("grp", None, "blk", None),
        P("blk", None),
        P("blk", None),
        P("blk", None),
        P("blk", None),
        P("blk"),
        P("blk", None),
        P("blk", None),
        P("blk", None),
        P("blk", None),
        P("blk"),
        P("grp", "blk", None),
        P("grp", "blk", None),
        P("grp", "blk", None),
        P("grp", "blk", None),
        P("blk", None, None),
        P("blk", None, None),
        P("blk", None, None),
        P("blk", None, None),
    )
    out_specs = (
        P("grp", None, "blk", None),
        P("grp", None, "blk", None),
        P("grp", "blk", None),
        P("grp", "blk", None),
        P("grp", "blk", None),
        P("grp", "blk", None),
        P("grp", "blk"),
        P("blk", None),
        P("blk", None),
        P("blk", None),
        P("blk", None),
        P("blk", None, None),
        P("blk", None, None),
        P("blk", None, None),
        P("blk", None, None),
        P("grp", "blk", None),
        P("grp", "blk", None),
        P("grp", "blk", None),
        P("grp", "blk", None),
        P("blk", None),
        P("blk", None),
        P("blk", None),
        P("blk", None),
        P("blk"),
        P("blk", None),
        P("blk", None),
        P("blk", None),
        P("blk", None),
        P("blk"),
        P("blk", None),
        P("blk", None),
        P("blk", None),
        P("blk", None),
        P("blk"),
    )

    return jax.shard_map(
        on_device, mesh=mesh, in_specs=in_specs, out_specs=out_specs, check_vma=False
    )
```
